32 devices in a mesh: gz: 8 (over z, core), grp: 4 (over y, x).
Axes of the slice: x: 2, y: 2, z: 4, core: 2. Of those that a mesh axis runs over, the one named last changes fastest.
Arguments:
- volumes: bfloat16 [4, 16, 16, 1024], P('grp', 'gz'), may hold values from -6 to 6
- cotangent: bfloat16 [4, 8, 64, 128], P(None, 'gz', None, 'grp'), may hold values from -6 to 6
- fine_kernel: bfloat16 [1728, 64], replicated, may hold values from -0.15625 to 0.15625
- down_kernel: bfloat16 [512, 128], replicated, may hold values from -0.25 to 0.25
- coarse_kernel: bfloat16 [3456, 128], P(None, 'grp'), may hold values from -0.109375 to 0.109375
Outputs:
- coarse_out: bfloat16 [4, 8, 64, 128], P(None, 'gz', None, 'grp')
- volume_grad: bfloat16 [4, 16, 16, 1024], P('grp', 'gz')
- fine_kernel_grad: float32 [1728, 64], replicated
- down_kernel_grad: float32 [512, 128], replicated
- coarse_kernel_grad: float32 [3456, 128], P(None, 'grp')
The draws below stay inside these ranges and needn't reach their ends.
All inputs are finite; a program needn't handle non-finite values.
Results may differ from the reference program's by a relative error of at most 0.019.
Values may be sent and summed in bfloat16 or wider, within the bound.
A program may use at most 64 MiB of HBM per device.

```python
import jax
import jax.numpy as jnp
from jax import lax

CFINE = 64
CCOARSE = 128
XFINE = 16
YFINE = 16
SAMPLES = 4
ZFINE = 16
ZCOARSE = 8
XYCOARSE = 64


def levels(rng, dims, cuts, smallest, high):
    def one(position, blocks):
        draws = jax.random.uniform(jax.random.fold_in(jax.random.fold_in(rng, 6), position), (blocks,), jnp.float32, smallest / len(cuts), high / len(cuts))
        return jnp.repeat(jnp.exp(draws), dims[position] // blocks).reshape((-1,) + (1,) * (len(dims) - position - 1))

    level = one(*cuts[0])
    for cut in cuts[1:]:
        level = level * one(*cut)
    return level


def bell_draw(own_key, extent, width, most, cuts=(), kind=jnp.bfloat16):
    drawn = jax.random.normal(own_key, extent, jnp.float32) * width
    if len(cuts) > 0:
        drawn = levels(own_key, extent, cuts, -0.22, 0.18) * drawn
    return jnp.clip(drawn, min=-most, max=most).astype(kind)


def setup_inputs(seed: int = 0) -> dict:
    arg_keys = jax.random.split(jax.random.key(seed), 6)
    volumes = bell_draw(arg_keys[0], (SAMPLES, ZFINE, XFINE, YFINE * CFINE), 1.0, 6.0, ((0, 4), (1, 8)))
    cotangent = bell_draw(arg_keys[1], (SAMPLES, ZCOARSE, XYCOARSE, CCOARSE), 1.0, 6.0, ((1, 8), (3, 4)))
    fine_kernel = bell_draw(arg_keys[2], (27 * CFINE, CFINE), (27 * CFINE) ** -0.5, 0.15625)
    down_kernel = bell_draw(arg_keys[3], (8 * CFINE, CCOARSE), (8 * CFINE) ** -0.5, 0.25)
    coarse_kernel = bell_draw(arg_keys[4], (27 * CCOARSE, CCOARSE), (27 * CCOARSE) ** -0.5, 0.109375, ((1, 4),))
    return {"volumes": volumes, "cotangent": cotangent, "fine_kernel": fine_kernel, "down_kernel": down_kernel, "coarse_kernel": coarse_kernel}


def pad_sides(block):
    return jnp.pad(block, ((0, 0), (1, 1), (1, 1), (1, 1), (0, 0)))


def convolve(padded, kernel):
    samples, extent_z, extent_x, extent_y, channels = padded.shape
    extent_z, extent_x, extent_y = extent_z - 2, extent_x - 2, extent_y - 2
    summed = None
    for plane in range(3):
        pieces = [padded[:, plane:plane + extent_z, row_step:row_step + extent_x, col_step:col_step + extent_y, :]
                  for row_step in range(3) for col_step in range(3)]
        columns = jnp.concatenate(pieces, axis=-1).reshape(-1, 9 * channels)
        rows = kernel[plane * 9 * channels:(plane + 1) * 9 * channels]
        partial_value = jnp.dot(columns, rows, preferred_element_type=jnp.float32)
        summed = partial_value if summed is None else summed + partial_value
    return summed.reshape(samples, extent_z, extent_x, extent_y, -1)


def kernel_gradient(padded, grad):
    samples, extent_z, extent_x, extent_y, channels = padded.shape
    extent_z, extent_x, extent_y = extent_z - 2, extent_x - 2, extent_y - 2
    flat_grad = grad.reshape(-1, grad.shape[-1])
    blocks = []
    for plane in range(3):
        pieces = [padded[:, plane:plane + extent_z, row_step:row_step + extent_x, col_step:col_step + extent_y, :]
                  for row_step in range(3) for col_step in range(3)]
        columns = jnp.concatenate(pieces, axis=-1).reshape(-1, 9 * channels)
        blocks.append(lax.dot_general(columns, flat_grad, (((0,), (0,)), ((), ())), preferred_element_type=jnp.float32))
    return jnp.concatenate(blocks, axis=0)


def flip_kernel(kernel, inputs):
    outputs = kernel.shape[1]
    shaped = kernel.reshape(3, 3, 3, inputs, outputs)[::-1, ::-1, ::-1]
    return jnp.transpose(shaped, (0, 1, 2, 4, 3)).reshape(27 * outputs, inputs)


def silu_slope(value):
    sigmoid_v = jax.nn.sigmoid(value)
    return sigmoid_v * (1.0 + value * (1.0 - sigmoid_v))


def pool_columns(block):
    samples, extent_z, extent_x, extent_y, channels = block.shape
    shaped = block.reshape(samples, extent_z // 2, 2, extent_x // 2, 2, extent_y // 2, 2, channels)
    return jnp.transpose(shaped, (0, 1, 3, 5, 2, 4, 6, 7)).reshape(-1, 8 * channels)


def unpool_columns(flat, samples, extent_z, extent_x, extent_y, channels):
    shaped = flat.reshape(samples, extent_z // 2, extent_x // 2, extent_y // 2, 2, 2, 2, channels)
    return jnp.transpose(shaped, (0, 1, 4, 2, 5, 3, 6, 7)).reshape(samples, extent_z, extent_x, extent_y, channels)


def one_volume(volume, grad_out, fine_kernel, down_kernel, coarse_kernel):
    cfine = fine_kernel.shape[1]
    extent_z, extent_x, packed = volume.shape
    extent_y = packed // cfine
    fine = volume.reshape(1, extent_z, extent_x, extent_y, cfine)
    fine_padded = pad_sides(fine)
    fine_pre = convolve(fine_padded, fine_kernel)
    fine_act = jax.nn.silu(fine_pre).astype(jnp.bfloat16)
    pooled = pool_columns(fine_act)
    coarse_in = jnp.dot(pooled, down_kernel, preferred_element_type=jnp.float32).astype(jnp.bfloat16)
    coarse_in = coarse_in.reshape(1, extent_z // 2, extent_x // 2, extent_y // 2, -1)
    coarse_padded = pad_sides(coarse_in)
    coarse_pre = convolve(coarse_padded, coarse_kernel)
    coarse_out = jax.nn.silu(coarse_pre).astype(jnp.bfloat16)
    grad_shaped = grad_out.reshape(coarse_pre.shape).astype(jnp.float32)
    coarse_grad = (grad_shaped * silu_slope(coarse_pre)).astype(jnp.bfloat16)
    coarse_kg = kernel_gradient(coarse_padded, coarse_grad)
    coarse_in_grad = convolve(pad_sides(coarse_grad), flip_kernel(coarse_kernel, coarse_kernel.shape[1])).astype(jnp.bfloat16)
    flat_in_grad = coarse_in_grad.reshape(-1, coarse_in_grad.shape[-1])
    pooled_grad = jnp.dot(flat_in_grad, down_kernel.T, preferred_element_type=jnp.float32)
    fine_act_grad = unpool_columns(pooled_grad, 1, extent_z, extent_x, extent_y, cfine)
    down_kg = lax.dot_general(pooled, flat_in_grad, (((0,), (0,)), ((), ())), preferred_element_type=jnp.float32)
    fine_grad = (fine_act_grad * silu_slope(fine_pre)).astype(jnp.bfloat16)
    fine_kg = kernel_gradient(fine_padded, fine_grad)
    volume_grad = convolve(pad_sides(fine_grad), flip_kernel(fine_kernel, cfine)).astype(jnp.bfloat16)
    out_flat = coarse_out.reshape(extent_z // 2, (extent_x // 2) * (extent_y // 2), -1)
    return out_flat, volume_grad.reshape(extent_z, extent_x, packed), fine_kg, down_kg, coarse_kg


def reference(volumes, cotangent, fine_kernel, down_kernel, coarse_kernel):
    def step(carry, inputs):
        volume, grad_out = inputs
        out_flat, volume_grad, fine_kg, down_kg, coarse_kg = one_volume(volume, grad_out, fine_kernel, down_kernel, coarse_kernel)
        carry = (carry[0] + fine_kg, carry[1] + down_kg, carry[2] + coarse_kg)
        return carry, (out_flat, volume_grad)

    start = (jnp.zeros(fine_kernel.shape, jnp.float32), jnp.zeros(down_kernel.shape, jnp.float32),
             jnp.zeros(coarse_kernel.shape, jnp.float32))
    sums, stacked = lax.scan(step, start, (volumes, cotangent))
    return stacked[0], stacked[1], sums[0], sums[1], sums[2]
```

```python
import functools

import jax
import jax.numpy as jnp
from jax import lax
from jax.experimental import pallas as pl
from jax.experimental.pallas import tpu as pltpu
from jax.sharding import PartitionSpec as P


def with_halo(array, sides, width):
    for axis, dim in sides:
        devices, length = (lax.axis_size(axis), array.shape[dim])
        up = [(i, (i + 1) % devices) for i in range(devices - 1)]
        down = [(j, i) for i, j in up]
        last = lax.slice_in_dim(array, length - width, length, axis=dim)
        initial = lax.slice_in_dim(array, 0, width, axis=dim)
        before = lax.ppermute(last, axis, up)
        after = lax.ppermute(initial, axis, down)
        array = jnp.concatenate([before, array, after], axis=dim)
    return array


def pad_sides(block):
    return jnp.pad(block, ((0, 0), (0, 0), (1, 1), (1, 1), (0, 0)))


def convolve(padded, kernel):
    samples, extent_z, extent_x, extent_y, channels = padded.shape
    extent_z, extent_x, extent_y = (extent_z - 2, extent_x - 2, extent_y - 2)
    summed = None
    for plane in range(3):
        pieces = [
            padded[
                :,
                plane : plane + extent_z,
                row_step : row_step + extent_x,
                col_step : col_step + extent_y,
                :,
            ]
            for row_step in range(3)
            for col_step in range(3)
        ]
        columns = jnp.concatenate(pieces, axis=-1).reshape(-1, 9 * channels)
        rows = kernel[plane * 9 * channels : (plane + 1) * 9 * channels]
        partial_value = jnp.dot(columns, rows, preferred_element_type=jnp.float32)
        summed = partial_value if summed is None else summed + partial_value
    return summed.reshape(samples, extent_z, extent_x, extent_y, -1)


def kernel_gradient(padded, grad):
    samples, extent_z, extent_x, extent_y, channels = padded.shape
    extent_z, extent_x, extent_y = (extent_z - 2, extent_x - 2, extent_y - 2)
    flat_grad = grad.reshape(-1, grad.shape[-1])
    blocks = []
    for plane in range(3):
        pieces = [
            padded[
                :,
                plane : plane + extent_z,
                row_step : row_step + extent_x,
                col_step : col_step + extent_y,
                :,
            ]
            for row_step in range(3)
            for col_step in range(3)
        ]
        columns = jnp.concatenate(pieces, axis=-1).reshape(-1, 9 * channels)
        blocks.append(
            lax.dot_general(
                columns, flat_grad, (((0,), (0,)), ((), ())), preferred_element_type=jnp.float32
            )
        )
    return jnp.concatenate(blocks, axis=0)


def flip_kernel(kernel, inputs):
    outputs = kernel.shape[1]
    shaped = kernel.reshape(3, 3, 3, inputs, outputs)[::-1, ::-1, ::-1]
    return jnp.transpose(shaped, (0, 1, 2, 4, 3)).reshape(27 * outputs, inputs)


def silu_slope(value):
    sigmoid_v = jax.nn.sigmoid(value)
    return sigmoid_v * (1.0 + value * (1.0 - sigmoid_v))


def pool_columns(block):
    samples, extent_z, extent_x, extent_y, channels = block.shape
    shaped = block.reshape(samples, extent_z // 2, 2, extent_x // 2, 2, extent_y // 2, 2, channels)
    return jnp.transpose(shaped, (0, 1, 3, 5, 2, 4, 6, 7)).reshape(-1, 8 * channels)


def unpool_columns(flat, samples, extent_z, extent_x, extent_y, channels):
    shaped = flat.reshape(samples, extent_z // 2, extent_x // 2, extent_y // 2, 2, 2, 2, channels)
    return jnp.transpose(shaped, (0, 1, 4, 2, 5, 3, 6, 7)).reshape(
        samples, extent_z, extent_x, extent_y, channels
    )


def coarse_rim(block):
    return with_halo(block, (("gz", 1),), 1)


def coarse_grad_rim(block):
    return with_halo(block, (("gz", 1),), 1)


MESH = pl.DeviceIdType.MESH


def exchange(src, dst, sends, recvs, slot, peer):
    return pltpu.make_async_remote_copy(
        src_ref=src,
        dst_ref=dst,
        send_sem=sends.at[slot],
        recv_sem=recvs.at[slot],
        device_id=peer,
        device_id_type=MESH,
    )


def totals_kernel(
    groups,
    slabs,
    both_ref,
    slab_ref,
    both_out,
    slab_out,
    grp_in,
    grp_sum,
    gz_in,
    both_all,
    slab_in,
    slab_all,
    grp_send,
    grp_recv,
    gz_send,
    gz_recv,
    slab_send,
    slab_recv,
):
    z = lax.axis_index("gz")
    g = lax.axis_index("grp")

    def at_gz(step):
        return lax.rem(z + step, slabs)

    def at_grp(step):
        return lax.rem(g + step, groups)

    barrier = pltpu.get_barrier_semaphore()
    for step in range(1, slabs):
        pl.semaphore_signal(barrier, inc=1, device_id=(at_gz(step), g), device_id_type=MESH)
    for step in range(1, groups):
        pl.semaphore_signal(barrier, inc=1, device_id=(z, at_grp(step)), device_id_type=MESH)
    pl.semaphore_wait(barrier, slabs + groups - 2)

    def run(copies):
        for copy in copies:
            copy.start()
        return copies

    def finish(copies):
        for copy in copies:
            copy.wait()

    first = run(
        [
            exchange(
                both_ref.at[at_grp(k)], grp_in.at[k - 1], grp_send.at[0], grp_recv.at[0], k - 1,
                (z, at_grp(k)),
            )
            for k in range(1, groups)
        ]
    )
    slab_first = run(
        [
            exchange(
                slab_ref.at[at_gz(k)], slab_in.at[k - 1], slab_send.at[0], slab_recv.at[0], k - 1,
                (at_gz(k), g),
            )
            for k in range(1, slabs)
        ]
    )
    finish(first)
    total = both_ref[g].astype(jnp.float32)
    for k in range(groups - 1):
        total = total + grp_in[k].astype(jnp.float32)
    grp_sum[...] = total.astype(jnp.bfloat16)
    second = run(
        [
            exchange(
                grp_sum.at[at_gz(k)], gz_in.at[k - 1], gz_send.at[0], gz_recv.at[0], k - 1,
                (at_gz(k), g),
            )
            for k in range(1, slabs)
        ]
    )
    finish(slab_first)
    slab_total = slab_ref[z].astype(jnp.float32)
    for k in range(slabs - 1):
        slab_total = slab_total + slab_in[k].astype(jnp.float32)
    slab_all[z] = slab_total.astype(jnp.bfloat16)
    finish(second)
    own = grp_sum[z].astype(jnp.float32)
    for k in range(slabs - 1):
        own = own + gz_in[k].astype(jnp.float32)
    both_all[g, z] = own.astype(jnp.bfloat16)
    third = run(
        [
            exchange(
                both_all.at[g, z], both_all.at[g, z], gz_send.at[1], gz_recv.at[1], k - 1,
                (at_gz(k), g),
            )
            for k in range(1, slabs)
        ]
    )
    slab_second = run(
        [
            exchange(
                slab_all.at[z], slab_all.at[z], slab_send.at[1], slab_recv.at[1], k - 1,
                (at_gz(k), g),
            )
            for k in range(1, slabs)
        ]
    )
    finish(third)
    fourth = run(
        [
            exchange(
                both_all.at[g], both_all.at[g], grp_send.at[1], grp_recv.at[1], k - 1,
                (z, at_grp(k)),
            )
            for k in range(1, groups)
        ]
    )
    finish(slab_second)
    slab_out[...] = slab_all[...].astype(jnp.float32)
    finish(fourth)
    both_out[...] = both_all[...].astype(jnp.float32)


def to_rows(array):
    fold = max(1, 128 // array.shape[1])
    rows = array.shape[0] // fold
    parts = [array[k * rows : (k + 1) * rows] for k in range(fold)]
    return jnp.concatenate(parts, axis=1) if fold > 1 else array


def from_rows(rows, shape):
    fold = max(1, 128 // shape[1])
    width = shape[1]
    parts = [rows[:, k * width : (k + 1) * width] for k in range(fold)]
    return jnp.concatenate(parts, axis=0) if fold > 1 else rows


def pad_rows(rows, pieces):
    depth = -(-rows.shape[0] // (pieces * 16)) * 16
    return jnp.pad(rows, ((0, pieces * depth - rows.shape[0]), (0, 0))), depth


def kernel_totals(fine_kg, down_kg, coarse_kg):
    slabs, groups = lax.axis_size("gz"), lax.axis_size("grp")
    fine_rows = to_rows(fine_kg.astype(jnp.bfloat16))
    down_rows = to_rows(down_kg.astype(jnp.bfloat16))
    coarse_rows = to_rows(coarse_kg.astype(jnp.bfloat16))
    fine_count, down_count, coarse_count = (
        fine_rows.shape[0], down_rows.shape[0], coarse_rows.shape[0],
    )
    both, depth = pad_rows(jnp.concatenate([fine_rows, down_rows], axis=0), slabs * groups)
    slab, slab_depth = pad_rows(coarse_rows, slabs)
    both = both.reshape(groups, slabs, depth, 128)
    slab = slab.reshape(slabs, slab_depth, 128)
    vmem = pl.BlockSpec(memory_space=pltpu.VMEM)
    dma = pltpu.SemaphoreType.DMA
    both, slab = pl.pallas_call(
        functools.partial(totals_kernel, groups, slabs),
        out_shape=(
            jax.ShapeDtypeStruct(both.shape, jnp.float32),
            jax.ShapeDtypeStruct(slab.shape, jnp.float32),
        ),
        in_specs=[vmem, vmem],
        out_specs=(vmem, vmem),
        scratch_shapes=[
            pltpu.VMEM((groups - 1, slabs, depth, 128), jnp.bfloat16),
            pltpu.VMEM((slabs, depth, 128), jnp.bfloat16),
            pltpu.VMEM((slabs - 1, depth, 128), jnp.bfloat16),
            pltpu.VMEM(both.shape, jnp.bfloat16),
            pltpu.VMEM((slabs - 1, slab_depth, 128), jnp.bfloat16),
            pltpu.VMEM(slab.shape, jnp.bfloat16),
            dma((2, groups - 1)),
            dma((2, groups - 1)),
            dma((2, slabs - 1)),
            dma((2, slabs - 1)),
            dma((2, slabs - 1)),
            dma((2, slabs - 1)),
        ],
        compiler_params=pltpu.CompilerParams(collective_id=0, has_side_effects=True),
    )(both, slab)
    both, slab = both.reshape(-1, 128), slab.reshape(-1, 128)
    return (
        from_rows(both[:fine_count], fine_kg.shape),
        from_rows(both[fine_count : fine_count + down_count], down_kg.shape),
        from_rows(slab[:coarse_count], coarse_kg.shape),
    )


def per_device(volumes, cotangent, fine_kernel, down_kernel, coarse_kernel):
    samples, planes, xfine, packed = volumes.shape
    cfine = fine_kernel.shape[1]
    yfine = packed // cfine
    fine = volumes.reshape(samples, planes, xfine, yfine, cfine)
    fine_padded = pad_sides(with_halo(fine, (("gz", 1),), 1))
    fine_pre = convolve(fine_padded, fine_kernel)
    fine_act = jax.nn.silu(fine_pre).astype(jnp.bfloat16)
    pooled = pool_columns(fine_act)
    coarse_in = jnp.dot(pooled, down_kernel, preferred_element_type=jnp.float32).astype(
        jnp.bfloat16
    )
    coarse_in = coarse_in.reshape(samples, planes // 2, xfine // 2, yfine // 2, -1)
    coarse_framed = coarse_rim(coarse_in)
    gathered = pad_sides(lax.all_gather(coarse_framed, "grp", axis=0, tiled=True))
    coarse_pre = convolve(gathered, coarse_kernel)
    group, zcoarse, xcoarse, ycoarse, own_channels = coarse_pre.shape
    coarse_out = (
        jax.nn.silu(coarse_pre)
        .astype(jnp.bfloat16)
        .reshape(group, zcoarse, xcoarse * ycoarse, own_channels)
    )
    grad_shaped = cotangent.reshape(coarse_pre.shape).astype(jnp.float32)
    coarse_grad = (grad_shaped * silu_slope(coarse_pre)).astype(jnp.bfloat16)
    coarse_kg = kernel_gradient(gathered, coarse_grad)
    partial_value = convolve(
        pad_sides(coarse_grad_rim(coarse_grad)),
        flip_kernel(coarse_kernel, coarse_kernel.shape[0] // 27),
    )
    coarse_in_grad = lax.psum_scatter(
        partial_value.astype(jnp.bfloat16), "grp", scatter_dimension=0, tiled=True
    )
    flat_in_grad = coarse_in_grad.reshape(-1, coarse_in_grad.shape[-1])
    pooled_grad = jnp.dot(flat_in_grad, down_kernel.T, preferred_element_type=jnp.float32)
    fine_act_grad = unpool_columns(pooled_grad, samples, planes, xfine, yfine, cfine)
    down_kg = lax.dot_general(
        pooled, flat_in_grad, (((0,), (0,)), ((), ())), preferred_element_type=jnp.float32
    )
    fine_grad = (fine_act_grad * silu_slope(fine_pre)).astype(jnp.bfloat16)
    fine_kg = kernel_gradient(fine_padded, fine_grad)
    fine_kg, down_kg, coarse_kg = kernel_totals(fine_kg, down_kg, coarse_kg)
    grad_padded = pad_sides(with_halo(fine_grad, (("gz", 1),), 1))
    volume_grad = convolve(grad_padded, flip_kernel(fine_kernel, cfine)).astype(jnp.bfloat16)
    volume_grad = volume_grad.reshape(samples, planes, xfine, packed)
    return (coarse_out, volume_grad, fine_kg, down_kg, coarse_kg)


def solution(mesh):
    in_specs = (P("grp", "gz", None, None), P(None, "gz", None, "grp"), P(), P(), P(None, "grp"))
    out_specs = (P(None, "gz", None, "grp"), P("grp", "gz", None, None), P(), P(), P(None, "grp"))
    return jax.shard_map(
        per_device, mesh=mesh, in_specs=in_specs, out_specs=out_specs, check_vma=False
    )
```

```python
import functools

import jax
import jax.numpy as jnp
from jax import lax
from jax.experimental import pallas as pl
from jax.experimental.pallas import tpu as pltpu
from jax.sharding import PartitionSpec as P


def with_halo(array, sides, width):
    for axis, dim in sides:
        devices, length = (lax.axis_size(axis), array.shape[dim])
        up = [(i, (i + 1) % devices) for i in range(devices - 1)]
        down = [(j, i) for i, j in up]
        last = lax.slice_in_dim(array, length - width, length, axis=dim)
        initial = lax.slice_in_dim(array, 0, width, axis=dim)
        before = lax.ppermute(last, axis, up)
        after = lax.ppermute(initial, axis, down)
        array = jnp.concatenate([before, array, after], axis=dim)
    return array


def pad_sides(block):
    return jnp.pad(block, ((0, 0), (0, 0), (1, 1), (1, 1), (0, 0)))


def convolve(padded, kernel):
    samples, extent_z, extent_x, extent_y, channels = padded.shape
    extent_z, extent_x, extent_y = (extent_z - 2, extent_x - 2, extent_y - 2)
    summed = None
    for plane in range(3):
        pieces = [
            padded[
                :,
                plane : plane + extent_z,
                row_step : row_step + extent_x,
                col_step : col_step + extent_y,
                :,
            ]
            for row_step in range(3)
            for col_step in range(3)
        ]
        columns = jnp.concatenate(pieces, axis=-1).reshape(-1, 9 * channels)
        rows = kernel[plane * 9 * channels : (plane + 1) * 9 * channels]
        partial_value = jnp.dot(columns, rows, preferred_element_type=jnp.float32)
        summed = partial_value if summed is None else summed + partial_value
    return summed.reshape(samples, extent_z, extent_x, extent_y, -1)


def kernel_gradient(padded, grad):
    samples, extent_z, extent_x, extent_y, channels = padded.shape
    extent_z, extent_x, extent_y = (extent_z - 2, extent_x - 2, extent_y - 2)
    flat_grad = grad.reshape(-1, grad.shape[-1])
    blocks = []
    for plane in range(3):
        pieces = [
            padded[
                :,
                plane : plane + extent_z,
                row_step : row_step + extent_x,
                col_step : col_step + extent_y,
                :,
            ]
            for row_step in range(3)
            for col_step in range(3)
        ]
        columns = jnp.concatenate(pieces, axis=-1).reshape(-1, 9 * channels)
        blocks.append(
            lax.dot_general(
                columns, flat_grad, (((0,), (0,)), ((), ())), preferred_element_type=jnp.float32
            )
        )
    return jnp.concatenate(blocks, axis=0)


def flip_kernel(kernel, inputs):
    outputs = kernel.shape[1]
    shaped = kernel.reshape(3, 3, 3, inputs, outputs)[::-1, ::-1, ::-1]
    return jnp.transpose(shaped, (0, 1, 2, 4, 3)).reshape(27 * outputs, inputs)


def silu_slope(value):
    sigmoid_v = jax.nn.sigmoid(value)
    return sigmoid_v * (1.0 + value * (1.0 - sigmoid_v))


def pool_columns(block):
    samples, extent_z, extent_x, extent_y, channels = block.shape
    shaped = block.reshape(samples, extent_z // 2, 2, extent_x // 2, 2, extent_y // 2, 2, channels)
    return jnp.transpose(shaped, (0, 1, 3, 5, 2, 4, 6, 7)).reshape(-1, 8 * channels)


def unpool_columns(flat, samples, extent_z, extent_x, extent_y, channels):
    shaped = flat.reshape(samples, extent_z // 2, extent_x // 2, extent_y // 2, 2, 2, 2, channels)
    return jnp.transpose(shaped, (0, 1, 4, 2, 5, 3, 6, 7)).reshape(
        samples, extent_z, extent_x, extent_y, channels
    )


MESH = pl.DeviceIdType.MESH


def exchange(src, dst, sends, recvs, slot, peer):
    return pltpu.make_async_remote_copy(
        src_ref=src,
        dst_ref=dst,
        send_sem=sends.at[slot],
        recv_sem=recvs.at[slot],
        device_id=peer,
        device_id_type=MESH,
    )


def totals_kernel(
    groups,
    slabs,
    both_ref,
    slab_ref,
    both_out,
    slab_out,
    grp_in,
    grp_sum,
    gz_in,
    both_all,
    slab_in,
    slab_all,
    grp_send,
    grp_recv,
    gz_send,
    gz_recv,
    slab_send,
    slab_recv,
):
    z = lax.axis_index("gz")
    g = lax.axis_index("grp")

    def at_gz(step):
        return lax.rem(z + step, slabs)

    def at_grp(step):
        return lax.rem(g + step, groups)

    barrier = pltpu.get_barrier_semaphore()
    for step in range(1, slabs):
        pl.semaphore_signal(barrier, inc=1, device_id=(at_gz(step), g), device_id_type=MESH)
    for step in range(1, groups):
        pl.semaphore_signal(barrier, inc=1, device_id=(z, at_grp(step)), device_id_type=MESH)
    pl.semaphore_wait(barrier, slabs + groups - 2)

    def run(copies):
        for copy in copies:
            copy.start()
        return copies

    def finish(copies):
        for copy in copies:
            copy.wait()

    first = run(
        [
            exchange(
                both_ref.at[at_grp(k)], grp_in.at[k - 1], grp_send.at[0], grp_recv.at[0], k - 1,
                (z, at_grp(k)),
            )
            for k in range(1, groups)
        ]
    )
    slab_first = run(
        [
            exchange(
                slab_ref.at[at_gz(k)], slab_in.at[k - 1], slab_send.at[0], slab_recv.at[0], k - 1,
                (at_gz(k), g),
            )
            for k in range(1, slabs)
        ]
    )
    finish(first)
    total = both_ref[g].astype(jnp.float32)
    for k in range(groups - 1):
        total = total + grp_in[k].astype(jnp.float32)
    grp_sum[...] = total.astype(jnp.bfloat16)
    second = run(
        [
            exchange(
                grp_sum.at[at_gz(k)], gz_in.at[k - 1], gz_send.at[0], gz_recv.at[0], k - 1,
                (at_gz(k), g),
            )
            for k in range(1, slabs)
        ]
    )
    finish(slab_first)
    slab_total = slab_ref[z].astype(jnp.float32)
    for k in range(slabs - 1):
        slab_total = slab_total + slab_in[k].astype(jnp.float32)
    slab_all[z] = slab_total.astype(jnp.bfloat16)
    finish(second)
    own = grp_sum[z].astype(jnp.float32)
    for k in range(slabs - 1):
        own = own + gz_in[k].astype(jnp.float32)
    both_all[g, z] = own.astype(jnp.bfloat16)
    third = run(
        [
            exchange(
                both_all.at[g, z], both_all.at[g, z], gz_send.at[1], gz_recv.at[1], k - 1,
                (at_gz(k), g),
            )
            for k in range(1, slabs)
        ]
    )
    slab_second = run(
        [
            exchange(
                slab_all.at[z], slab_all.at[z], slab_send.at[1], slab_recv.at[1], k - 1,
                (at_gz(k), g),
            )
            for k in range(1, slabs)
        ]
    )
    finish(third)
    fourth = run(
        [
            exchange(
                both_all.at[g], both_all.at[g], grp_send.at[1], grp_recv.at[1], k - 1,
                (z, at_grp(k)),
            )
            for k in range(1, groups)
        ]
    )
    finish(slab_second)
    slab_out[...] = slab_all[...].astype(jnp.float32)
    finish(fourth)
    both_out[...] = both_all[...].astype(jnp.float32)


def to_rows(array):
    fold = max(1, 128 // array.shape[1])
    rows = array.shape[0] // fold
    parts = [array[k * rows : (k + 1) * rows] for k in range(fold)]
    return jnp.concatenate(parts, axis=1) if fold > 1 else array


def from_rows(rows, shape):
    fold = max(1, 128 // shape[1])
    width = shape[1]
    parts = [rows[:, k * width : (k + 1) * width] for k in range(fold)]
    return jnp.concatenate(parts, axis=0) if fold > 1 else rows


def pad_rows(rows, pieces):
    depth = -(-rows.shape[0] // (pieces * 16)) * 16
    return jnp.pad(rows, ((0, pieces * depth - rows.shape[0]), (0, 0))), depth


def kernel_totals(fine_kg, down_kg, coarse_kg):
    slabs, groups = lax.axis_size("gz"), lax.axis_size("grp")
    fine_rows = to_rows(fine_kg.astype(jnp.bfloat16))
    down_rows = to_rows(down_kg.astype(jnp.bfloat16))
    coarse_rows = to_rows(coarse_kg.astype(jnp.bfloat16))
    fine_count, down_count, coarse_count = (
        fine_rows.shape[0], down_rows.shape[0], coarse_rows.shape[0],
    )
    both, depth = pad_rows(jnp.concatenate([fine_rows, down_rows], axis=0), slabs * groups)
    slab, slab_depth = pad_rows(coarse_rows, slabs)
    both = both.reshape(groups, slabs, depth, 128)
    slab = slab.reshape(slabs, slab_depth, 128)
    vmem = pl.BlockSpec(memory_space=pltpu.VMEM)
    dma = pltpu.SemaphoreType.DMA
    both, slab = pl.pallas_call(
        functools.partial(totals_kernel, groups, slabs),
        out_shape=(
            jax.ShapeDtypeStruct(both.shape, jnp.float32),
            jax.ShapeDtypeStruct(slab.shape, jnp.float32),
        ),
        in_specs=[vmem, vmem],
        out_specs=(vmem, vmem),
        scratch_shapes=[
            pltpu.VMEM((groups - 1, slabs, depth, 128), jnp.bfloat16),
            pltpu.VMEM((slabs, depth, 128), jnp.bfloat16),
            pltpu.VMEM((slabs - 1, depth, 128), jnp.bfloat16),
            pltpu.VMEM(both.shape, jnp.bfloat16),
            pltpu.VMEM((slabs - 1, slab_depth, 128), jnp.bfloat16),
            pltpu.VMEM(slab.shape, jnp.bfloat16),
            dma((2, groups - 1)),
            dma((2, groups - 1)),
            dma((2, slabs - 1)),
            dma((2, slabs - 1)),
            dma((2, slabs - 1)),
            dma((2, slabs - 1)),
        ],
        compiler_params=pltpu.CompilerParams(collective_id=0, has_side_effects=True),
    )(both, slab)
    both, slab = both.reshape(-1, 128), slab.reshape(-1, 128)
    return (
        from_rows(both[:fine_count], fine_kg.shape),
        from_rows(both[fine_count : fine_count + down_count], down_kg.shape),
        from_rows(slab[:coarse_count], coarse_kg.shape),
    )


def spread_kernel(
    groups, slabs, shared, src_ref, out_ref, inbox, mid_send, mid_recv, up_send, up_recv, down_send,
    down_recv,
):
    z = lax.axis_index("gz")
    g = lax.axis_index("grp")
    planes = src_ref.shape[1]

    def at_grp(step):
        return lax.rem(g + step, groups)

    def block(step):
        return 0 if shared else at_grp(step)

    def greet(level, steps):
        for step in steps:
            pl.semaphore_signal(
                barrier, inc=1, device_id=(level, at_grp(step)), device_id_type=MESH
            )

    def middle(k):
        return exchange(
            src_ref.at[block(k)], inbox.at[g, pl.ds(1, planes)], mid_send, mid_recv, k - 1,
            (z, at_grp(k)),
        )

    def upward(k):
        return exchange(
            src_ref.at[block(k), planes - 1], inbox.at[g, 0], up_send, up_recv, k,
            (z + 1, at_grp(k)),
        )

    def downward(k):
        return exchange(
            src_ref.at[block(k), 0], inbox.at[g, planes + 1], down_send, down_recv, k,
            (z - 1, at_grp(k)),
        )

    barrier = pltpu.get_barrier_semaphore()
    below = z > 0
    above = z < slabs - 1
    greet(z, range(1, groups))

    @pl.when(below)
    def _():
        greet(z - 1, range(groups))

    @pl.when(above)
    def _():
        greet(z + 1, range(groups))

    sides = below.astype(jnp.int32) + above.astype(jnp.int32)
    pl.semaphore_wait(barrier, groups - 1 + groups * sides)

    @pl.when(above)
    def _():
        for k in range(groups):
            upward(k).start()

    @pl.when(below)
    def _():
        for k in range(groups):
            downward(k).start()

    for k in range(1, groups):
        middle(k).start()

    out_ref[g, pl.ds(1, planes)] = src_ref[block(0)]
    for k in range(1, groups):
        middle(k).wait()
        source = lax.rem(g + groups - k, groups)
        out_ref[source, pl.ds(1, planes)] = inbox[source, pl.ds(1, planes)]

    @pl.when(above)
    def _():
        for k in range(groups):
            upward(k).wait_send()
            downward(k).wait_recv()
        out_ref[:, planes + 1] = inbox[:, planes + 1]

    @pl.when(below)
    def _():
        for k in range(groups):
            downward(k).wait_send()
            upward(k).wait_recv()
        out_ref[:, 0] = inbox[:, 0]

    @pl.when(jnp.logical_not(above))
    def _():
        out_ref[:, planes + 1] = jnp.zeros_like(out_ref[:, planes + 1])

    @pl.when(jnp.logical_not(below))
    def _():
        out_ref[:, 0] = jnp.zeros_like(out_ref[:, 0])


def spread(blocks, number):
    slabs, groups = lax.axis_size("gz"), lax.axis_size("grp")
    shared = blocks.shape[0] == 1
    planes = blocks.shape[1]
    shape = (groups, planes + 2) + blocks.shape[2:]
    vmem = pl.BlockSpec(memory_space=pltpu.VMEM)
    dma = pltpu.SemaphoreType.DMA
    return pl.pallas_call(
        functools.partial(spread_kernel, groups, slabs, shared),
        out_shape=jax.ShapeDtypeStruct(shape, blocks.dtype),
        in_specs=[vmem],
        out_specs=vmem,
        scratch_shapes=[
            pltpu.VMEM(shape, blocks.dtype),
            dma((groups - 1,)),
            dma((groups - 1,)),
            dma((groups,)),
            dma((groups,)),
            dma((groups,)),
            dma((groups,)),
        ],
        compiler_params=pltpu.CompilerParams(collective_id=number, has_side_effects=True),
    )(blocks)


def per_device(volumes, cotangent, fine_kernel, down_kernel, coarse_kernel):
    samples, planes, xfine, packed = volumes.shape
    cfine = fine_kernel.shape[1]
    yfine = packed // cfine
    fine = volumes.reshape(samples, planes, xfine, yfine, cfine)
    local = flip_kernel(coarse_kernel, coarse_kernel.shape[0] // 27)
    flipped = lax.all_gather(
        local.reshape(27, coarse_kernel.shape[1], -1), "grp", axis=1, tiled=True
    ).reshape(coarse_kernel.shape[0], -1)
    fine_padded = pad_sides(with_halo(fine, (("gz", 1),), 1))
    fine_pre = convolve(fine_padded, fine_kernel)
    fine_act = jax.nn.silu(fine_pre).astype(jnp.bfloat16)
    pooled = pool_columns(fine_act)
    coarse_in = jnp.dot(pooled, down_kernel, preferred_element_type=jnp.float32).astype(
        jnp.bfloat16
    )
    coarse_in = coarse_in.reshape(samples, planes // 2, xfine // 2, yfine // 2, -1)
    planes_c, x_c, y_c, channels_c = coarse_in.shape[1:]
    gathered = pad_sides(
        lax.all_gather(with_halo(coarse_in, (("gz", 1),), 1), "grp", axis=0, tiled=True)
    )
    coarse_pre = convolve(gathered, coarse_kernel)
    group, zcoarse, xcoarse, ycoarse, own_channels = coarse_pre.shape
    coarse_out = (
        jax.nn.silu(coarse_pre)
        .astype(jnp.bfloat16)
        .reshape(group, zcoarse, xcoarse * ycoarse, own_channels)
    )
    grad_shaped = cotangent.reshape(coarse_pre.shape).astype(jnp.float32)
    coarse_grad = (grad_shaped * silu_slope(coarse_pre)).astype(jnp.bfloat16)
    coarse_kg = kernel_gradient(gathered, coarse_grad)
    groups = lax.axis_size("grp")
    to_send = coarse_grad.reshape(groups, samples, planes_c, x_c * y_c, own_channels)
    arrived = spread(jnp.swapaxes(to_send, 1, 2), 2)
    own_grad = jnp.transpose(arrived, (2, 1, 3, 0, 4)).reshape(
        samples, planes_c + 2, x_c, y_c, channels_c
    )
    coarse_in_grad = convolve(pad_sides(own_grad), flipped).astype(jnp.bfloat16)
    flat_in_grad = coarse_in_grad.reshape(-1, coarse_in_grad.shape[-1])
    pooled_grad = jnp.dot(flat_in_grad, down_kernel.T, preferred_element_type=jnp.float32)
    fine_act_grad = unpool_columns(pooled_grad, samples, planes, xfine, yfine, cfine)
    down_kg = lax.dot_general(
        pooled, flat_in_grad, (((0,), (0,)), ((), ())), preferred_element_type=jnp.float32
    )
    fine_grad = (fine_act_grad * silu_slope(fine_pre)).astype(jnp.bfloat16)
    fine_kg = kernel_gradient(fine_padded, fine_grad)
    fine_kg, down_kg, coarse_kg = kernel_totals(fine_kg, down_kg, coarse_kg)
    grad_padded = pad_sides(with_halo(fine_grad, (("gz", 1),), 1))
    volume_grad = convolve(grad_padded, flip_kernel(fine_kernel, cfine)).astype(jnp.bfloat16)
    volume_grad = volume_grad.reshape(samples, planes, xfine, packed)
    return (coarse_out, volume_grad, fine_kg, down_kg, coarse_kg)


def solution(mesh):
    in_specs = (P("grp", "gz", None, None), P(None, "gz", None, "grp"), P(), P(), P(None, "grp"))
    out_specs = (P(None, "gz", None, "grp"), P("grp", "gz", None, None), P(), P(), P(None, "grp"))
    return jax.shard_map(
        per_device, mesh=mesh, in_specs=in_specs, out_specs=out_specs, check_vma=False
    )
```

```python
import functools

import jax
import jax.numpy as jnp
from jax import lax
from jax.experimental import pallas as pl
from jax.experimental.pallas import tpu as pltpu
from jax.sharding import PartitionSpec as P


def with_halo(array, sides, width):
    for axis, dim in sides:
        devices, length = (lax.axis_size(axis), array.shape[dim])
        up = [(i, (i + 1) % devices) for i in range(devices - 1)]
        down = [(j, i) for i, j in up]
        last = lax.slice_in_dim(array, length - width, length, axis=dim)
        initial = lax.slice_in_dim(array, 0, width, axis=dim)
        before = lax.ppermute(last, axis, up)
        after = lax.ppermute(initial, axis, down)
        array = jnp.concatenate([before, array, after], axis=dim)
    return array


def pad_sides(block):
    return jnp.pad(block, ((0, 0), (0, 0), (1, 1), (1, 1), (0, 0)))


def convolve(padded, kernel):
    samples, extent_z, extent_x, extent_y, channels = padded.shape
    extent_z, extent_x, extent_y = (extent_z - 2, extent_x - 2, extent_y - 2)
    summed = None
    for plane in range(3):
        pieces = [
            padded[
                :,
                plane : plane + extent_z,
                row_step : row_step + extent_x,
                col_step : col_step + extent_y,
                :,
            ]
            for row_step in range(3)
            for col_step in range(3)
        ]
        columns = jnp.concatenate(pieces, axis=-1).reshape(-1, 9 * channels)
        rows = kernel[plane * 9 * channels : (plane + 1) * 9 * channels]
        partial_value = jnp.dot(columns, rows, preferred_element_type=jnp.float32)
        summed = partial_value if summed is None else summed + partial_value
    return summed.reshape(samples, extent_z, extent_x, extent_y, -1)


def kernel_gradient(padded, grad):
    samples, extent_z, extent_x, extent_y, channels = padded.shape
    extent_z, extent_x, extent_y = (extent_z - 2, extent_x - 2, extent_y - 2)
    flat_grad = grad.reshape(-1, grad.shape[-1])
    blocks = []
    for plane in range(3):
        pieces = [
            padded[
                :,
                plane : plane + extent_z,
                row_step : row_step + extent_x,
                col_step : col_step + extent_y,
                :,
            ]
            for row_step in range(3)
            for col_step in range(3)
        ]
        columns = jnp.concatenate(pieces, axis=-1).reshape(-1, 9 * channels)
        blocks.append(
            lax.dot_general(
                columns, flat_grad, (((0,), (0,)), ((), ())), preferred_element_type=jnp.float32
            )
        )
    return jnp.concatenate(blocks, axis=0)


def flip_kernel(kernel, inputs):
    outputs = kernel.shape[1]
    shaped = kernel.reshape(3, 3, 3, inputs, outputs)[::-1, ::-1, ::-1]
    return jnp.transpose(shaped, (0, 1, 2, 4, 3)).reshape(27 * outputs, inputs)


def silu_slope(value):
    sigmoid_v = jax.nn.sigmoid(value)
    return sigmoid_v * (1.0 + value * (1.0 - sigmoid_v))


def pool_columns(block):
    samples, extent_z, extent_x, extent_y, channels = block.shape
    shaped = block.reshape(samples, extent_z // 2, 2, extent_x // 2, 2, extent_y // 2, 2, channels)
    return jnp.transpose(shaped, (0, 1, 3, 5, 2, 4, 6, 7)).reshape(-1, 8 * channels)


def unpool_columns(flat, samples, extent_z, extent_x, extent_y, channels):
    shaped = flat.reshape(samples, extent_z // 2, extent_x // 2, extent_y // 2, 2, 2, 2, channels)
    return jnp.transpose(shaped, (0, 1, 4, 2, 5, 3, 6, 7)).reshape(
        samples, extent_z, extent_x, extent_y, channels
    )


MESH = pl.DeviceIdType.MESH


def exchange(src, dst, sends, recvs, slot, peer):
    return pltpu.make_async_remote_copy(
        src_ref=src,
        dst_ref=dst,
        send_sem=sends.at[slot],
        recv_sem=recvs.at[slot],
        device_id=peer,
        device_id_type=MESH,
    )


def totals_kernel(
    groups,
    slabs,
    both_ref,
    slab_ref,
    both_out,
    slab_out,
    grp_in,
    grp_sum,
    gz_in,
    both_all,
    slab_in,
    slab_all,
    grp_send,
    grp_recv,
    gz_send,
    gz_recv,
    slab_send,
    slab_recv,
):
    z = lax.axis_index("gz")
    g = lax.axis_index("grp")

    def at_gz(step):
        return lax.rem(z + step, slabs)

    def at_grp(step):
        return lax.rem(g + step, groups)

    barrier = pltpu.get_barrier_semaphore()
    for step in range(1, slabs):
        pl.semaphore_signal(barrier, inc=1, device_id=(at_gz(step), g), device_id_type=MESH)
    for step in range(1, groups):
        pl.semaphore_signal(barrier, inc=1, device_id=(z, at_grp(step)), device_id_type=MESH)
    pl.semaphore_wait(barrier, slabs + groups - 2)

    def run(copies):
        for copy in copies:
            copy.start()
        return copies

    def finish(copies):
        for copy in copies:
            copy.wait()

    first = run(
        [
            exchange(
                both_ref.at[at_grp(k)], grp_in.at[k - 1], grp_send.at[0], grp_recv.at[0], k - 1,
                (z, at_grp(k)),
            )
            for k in range(1, groups)
        ]
    )
    slab_first = run(
        [
            exchange(
                slab_ref.at[at_gz(k)], slab_in.at[k - 1], slab_send.at[0], slab_recv.at[0], k - 1,
                (at_gz(k), g),
            )
            for k in range(1, slabs)
        ]
    )
    finish(first)
    total = both_ref[g].astype(jnp.float32)
    for k in range(groups - 1):
        total = total + grp_in[k].astype(jnp.float32)
    grp_sum[...] = total.astype(jnp.bfloat16)
    second = run(
        [
            exchange(
                grp_sum.at[at_gz(k)], gz_in.at[k - 1], gz_send.at[0], gz_recv.at[0], k - 1,
                (at_gz(k), g),
            )
            for k in range(1, slabs)
        ]
    )
    finish(slab_first)
    slab_total = slab_ref[z].astype(jnp.float32)
    for k in range(slabs - 1):
        slab_total = slab_total + slab_in[k].astype(jnp.float32)
    slab_all[z] = slab_total.astype(jnp.bfloat16)
    finish(second)
    own = grp_sum[z].astype(jnp.float32)
    for k in range(slabs - 1):
        own = own + gz_in[k].astype(jnp.float32)
    both_all[g, z] = own.astype(jnp.bfloat16)
    third = run(
        [
            exchange(
                both_all.at[g, z], both_all.at[g, z], gz_send.at[1], gz_recv.at[1], k - 1,
                (at_gz(k), g),
            )
            for k in range(1, slabs)
        ]
    )
    slab_second = run(
        [
            exchange(
                slab_all.at[z], slab_all.at[z], slab_send.at[1], slab_recv.at[1], k - 1,
                (at_gz(k), g),
            )
            for k in range(1, slabs)
        ]
    )
    finish(third)
    fourth = run(
        [
            exchange(
                both_all.at[g], both_all.at[g], grp_send.at[1], grp_recv.at[1], k - 1,
                (z, at_grp(k)),
            )
            for k in range(1, groups)
        ]
    )
    finish(slab_second)
    slab_out[...] = slab_all[...].astype(jnp.float32)
    finish(fourth)
    both_out[...] = both_all[...].astype(jnp.float32)


def to_rows(array):
    fold = max(1, 128 // array.shape[1])
    rows = array.shape[0] // fold
    parts = [array[k * rows : (k + 1) * rows] for k in range(fold)]
    return jnp.concatenate(parts, axis=1) if fold > 1 else array


def from_rows(rows, shape):
    fold = max(1, 128 // shape[1])
    width = shape[1]
    parts = [rows[:, k * width : (k + 1) * width] for k in range(fold)]
    return jnp.concatenate(parts, axis=0) if fold > 1 else rows


def pad_rows(rows, pieces):
    depth = -(-rows.shape[0] // (pieces * 16)) * 16
    return jnp.pad(rows, ((0, pieces * depth - rows.shape[0]), (0, 0))), depth


def kernel_totals(fine_kg, down_kg, coarse_kg):
    slabs, groups = lax.axis_size("gz"), lax.axis_size("grp")
    fine_rows = to_rows(fine_kg.astype(jnp.bfloat16))
    down_rows = to_rows(down_kg.astype(jnp.bfloat16))
    coarse_rows = to_rows(coarse_kg.astype(jnp.bfloat16))
    fine_count, down_count, coarse_count = (
        fine_rows.shape[0], down_rows.shape[0], coarse_rows.shape[0],
    )
    both, depth = pad_rows(jnp.concatenate([fine_rows, down_rows], axis=0), slabs * groups)
    slab, slab_depth = pad_rows(coarse_rows, slabs)
    both = both.reshape(groups, slabs, depth, 128)
    slab = slab.reshape(slabs, slab_depth, 128)
    vmem = pl.BlockSpec(memory_space=pltpu.VMEM)
    dma = pltpu.SemaphoreType.DMA
    both, slab = pl.pallas_call(
        functools.partial(totals_kernel, groups, slabs),
        out_shape=(
            jax.ShapeDtypeStruct(both.shape, jnp.float32),
            jax.ShapeDtypeStruct(slab.shape, jnp.float32),
        ),
        in_specs=[vmem, vmem],
        out_specs=(vmem, vmem),
        scratch_shapes=[
            pltpu.VMEM((groups - 1, slabs, depth, 128), jnp.bfloat16),
            pltpu.VMEM((slabs, depth, 128), jnp.bfloat16),
            pltpu.VMEM((slabs - 1, depth, 128), jnp.bfloat16),
            pltpu.VMEM(both.shape, jnp.bfloat16),
            pltpu.VMEM((slabs - 1, slab_depth, 128), jnp.bfloat16),
            pltpu.VMEM(slab.shape, jnp.bfloat16),
            dma((2, groups - 1)),
            dma((2, groups - 1)),
            dma((2, slabs - 1)),
            dma((2, slabs - 1)),
            dma((2, slabs - 1)),
            dma((2, slabs - 1)),
        ],
        compiler_params=pltpu.CompilerParams(collective_id=0, has_side_effects=True),
    )(both, slab)
    both, slab = both.reshape(-1, 128), slab.reshape(-1, 128)
    return (
        from_rows(both[:fine_count], fine_kg.shape),
        from_rows(both[fine_count : fine_count + down_count], down_kg.shape),
        from_rows(slab[:coarse_count], coarse_kg.shape),
    )


def spread_kernel(
    groups, slabs, shared, src_ref, out_ref, inbox, mid_send, mid_recv, up_send, up_recv, down_send,
    down_recv,
):
    z = lax.axis_index("gz")
    g = lax.axis_index("grp")
    planes = src_ref.shape[1]

    def at_grp(step):
        return lax.rem(g + step, groups)

    def block(step):
        return 0 if shared else at_grp(step)

    def greet(level, steps):
        for step in steps:
            pl.semaphore_signal(
                barrier, inc=1, device_id=(level, at_grp(step)), device_id_type=MESH
            )

    def middle(k):
        return exchange(
            src_ref.at[block(k)], inbox.at[k, pl.ds(1, planes)], mid_send, mid_recv, k - 1,
            (z, at_grp(k)),
        )

    def upward(k):
        return exchange(
            src_ref.at[block(k), planes - 1], inbox.at[k, 0], up_send, up_recv, k,
            (z + 1, at_grp(k)),
        )

    def downward(k):
        return exchange(
            src_ref.at[block(k), 0], inbox.at[k, planes + 1], down_send, down_recv, k,
            (z - 1, at_grp(k)),
        )

    barrier = pltpu.get_barrier_semaphore()
    below = z > 0
    above = z < slabs - 1
    greet(z, range(1, groups))

    @pl.when(below)
    def _():
        greet(z - 1, range(groups))

    @pl.when(above)
    def _():
        greet(z + 1, range(groups))

    sides = below.astype(jnp.int32) + above.astype(jnp.int32)
    pl.semaphore_wait(barrier, groups - 1 + groups * sides)

    @pl.when(above)
    def _():
        for k in range(groups):
            upward(k).start()

    @pl.when(below)
    def _():
        for k in range(groups):
            downward(k).start()

    for k in range(1, groups):
        middle(k).start()

    out_ref[0, pl.ds(1, planes)] = src_ref[block(0)]
    for k in range(1, groups):
        middle(k).wait()
        out_ref[k, pl.ds(1, planes)] = inbox[k, pl.ds(1, planes)]

    @pl.when(above)
    def _():
        for k in range(groups):
            upward(k).wait_send()
            downward(k).wait_recv()
        out_ref[:, planes + 1] = inbox[:, planes + 1]

    @pl.when(below)
    def _():
        for k in range(groups):
            downward(k).wait_send()
            upward(k).wait_recv()
        out_ref[:, 0] = inbox[:, 0]

    @pl.when(jnp.logical_not(above))
    def _():
        out_ref[:, planes + 1] = jnp.zeros_like(out_ref[:, planes + 1])

    @pl.when(jnp.logical_not(below))
    def _():
        out_ref[:, 0] = jnp.zeros_like(out_ref[:, 0])


def spread(blocks, number):
    slabs, groups = lax.axis_size("gz"), lax.axis_size("grp")
    shared = blocks.shape[0] == 1
    planes = blocks.shape[1]
    shape = (groups, planes + 2) + blocks.shape[2:]
    vmem = pl.BlockSpec(memory_space=pltpu.VMEM)
    dma = pltpu.SemaphoreType.DMA
    return pl.pallas_call(
        functools.partial(spread_kernel, groups, slabs, shared),
        out_shape=jax.ShapeDtypeStruct(shape, blocks.dtype),
        in_specs=[vmem],
        out_specs=vmem,
        scratch_shapes=[
            pltpu.VMEM(shape, blocks.dtype),
            dma((groups - 1,)),
            dma((groups - 1,)),
            dma((groups,)),
            dma((groups,)),
            dma((groups,)),
            dma((groups,)),
        ],
        compiler_params=pltpu.CompilerParams(collective_id=number, has_side_effects=True),
    )(blocks)


def per_device(volumes, cotangent, fine_kernel, down_kernel, coarse_kernel):
    samples, planes, xfine, packed = volumes.shape
    cfine = fine_kernel.shape[1]
    yfine = packed // cfine
    fine = volumes.reshape(samples, planes, xfine, yfine, cfine)
    fine_padded = pad_sides(with_halo(fine, (("gz", 1),), 1))
    local = flip_kernel(coarse_kernel, coarse_kernel.shape[0] // 27)
    groups = lax.axis_size("grp")
    kernel_parts = [local] + [
        lax.ppermute(local, "grp", [(i, (i + step) % groups) for i in range(groups)])
        for step in range(1, groups)
    ]
    fine_pre = convolve(fine_padded, fine_kernel)
    fine_act = jax.nn.silu(fine_pre).astype(jnp.bfloat16)
    pooled = pool_columns(fine_act)
    coarse_in = jnp.dot(pooled, down_kernel, preferred_element_type=jnp.float32).astype(
        jnp.bfloat16
    )
    coarse_in = coarse_in.reshape(samples, planes // 2, xfine // 2, yfine // 2, -1)
    planes_c, x_c, y_c, channels_c = coarse_in.shape[1:]
    gathered = pad_sides(
        lax.all_gather(with_halo(coarse_in, (("gz", 1),), 1), "grp", axis=0, tiled=True)
    )
    coarse_pre = convolve(gathered, coarse_kernel)
    group, zcoarse, xcoarse, ycoarse, own_channels = coarse_pre.shape
    coarse_out = (
        jax.nn.silu(coarse_pre)
        .astype(jnp.bfloat16)
        .reshape(group, zcoarse, xcoarse * ycoarse, own_channels)
    )
    grad_shaped = cotangent.reshape(coarse_pre.shape).astype(jnp.float32)
    coarse_grad = (grad_shaped * silu_slope(coarse_pre)).astype(jnp.bfloat16)
    coarse_kg = kernel_gradient(gathered, coarse_grad)
    to_send = coarse_grad.reshape(groups, samples, planes_c, x_c * y_c, own_channels)
    arrived = spread(jnp.swapaxes(to_send, 1, 2), 2)
    own_grad = jnp.transpose(arrived, (2, 1, 3, 0, 4)).reshape(
        samples, planes_c + 2, x_c, y_c, channels_c
    )
    flipped = jnp.concatenate(
        [part.reshape(27, own_channels, channels_c) for part in kernel_parts], axis=1
    ).reshape(-1, channels_c)
    coarse_in_grad = convolve(pad_sides(own_grad), flipped).astype(jnp.bfloat16)
    flat_in_grad = coarse_in_grad.reshape(-1, coarse_in_grad.shape[-1])
    pooled_grad = jnp.dot(flat_in_grad, down_kernel.T, preferred_element_type=jnp.float32)
    fine_act_grad = unpool_columns(pooled_grad, samples, planes, xfine, yfine, cfine)
    down_kg = lax.dot_general(
        pooled, flat_in_grad, (((0,), (0,)), ((), ())), preferred_element_type=jnp.float32
    )
    fine_grad = (fine_act_grad * silu_slope(fine_pre)).astype(jnp.bfloat16)
    fine_kg = kernel_gradient(fine_padded, fine_grad)
    fine_kg, down_kg, coarse_kg = kernel_totals(fine_kg, down_kg, coarse_kg)
    grad_padded = pad_sides(with_halo(fine_grad, (("gz", 1),), 1))
    volume_grad = convolve(grad_padded, flip_kernel(fine_kernel, cfine)).astype(jnp.bfloat16)
    volume_grad = volume_grad.reshape(samples, planes, xfine, packed)
    return (coarse_out, volume_grad, fine_kg, down_kg, coarse_kg)


def solution(mesh):
    in_specs = (P("grp", "gz", None, None), P(None, "gz", None, "grp"), P(), P(), P(None, "grp"))
    out_specs = (P(None, "gz", None, "grp"), P("grp", "gz", None, None), P(), P(), P(None, "grp"))
    return jax.shard_map(
        per_device, mesh=mesh, in_specs=in_specs, out_specs=out_specs, check_vma=False
    )
```
